32 devices in a mesh: fsdp: 8 (over z, x), rep: 4 (over y, core).
Axes of the slice: x: 2, y: 2, z: 4, core: 2. Of those that a mesh axis runs over, the one named last changes fastest.
Arguments:
- latents: float32 [256, 256, 384], P(('fsdp', 'rep')), may hold values from -6 to 6
- condition: float32 [256, 384], P(('fsdp', 'rep')), may hold values from -6 to 6
- cotangent: float32 [256, 256, 384], P(('fsdp', 'rep')), may hold values from -6 to 6
- w_ada: bfloat16 [2, 384, 2304], P(None, 'fsdp'), may hold values from -0.3125 to 0.3125
- b_ada: bfloat16 [2, 2304], P(None, 'fsdp'), may hold values from -3 to 3
- w_qkv: bfloat16 [2, 384, 1152], P(None, 'fsdp'), may hold values from -0.3125 to 0.3125
- qv_bias: bfloat16 [2, 768], P(None, 'fsdp'), may hold values from -3 to 3
- w_out: bfloat16 [2, 384, 384], P(None, 'fsdp'), may hold values from -1.25 to 1.25
- b_out: bfloat16 [2, 384], P(None, 'fsdp'), may hold values from -3 to 3
- w_up: bfloat16 [2, 384, 1536], P(None, 'fsdp'), may hold values from -0.3125 to 0.3125
- b_up: bfloat16 [2, 1536], P(None, 'fsdp'), may hold values from -3 to 3
- w_down: bfloat16 [2, 1536, 384], P(None, 'fsdp'), may hold values from -0.15625 to 0.15625
- b_down: bfloat16 [2, 384], P(None, 'fsdp'), may hold values from -3 to 3
Outputs:
- output: float32 [256, 256, 384], P(('fsdp', 'rep'))
- grad_latents: float32 [256, 256, 384], P(('fsdp', 'rep'))
- grad_condition: float32 [256, 384], P(('fsdp', 'rep'))
- grad_w_ada: float32 [2, 384, 2304], P(None, 'fsdp')
- grad_b_ada: float32 [2, 2304], P(None, 'fsdp')
- grad_w_qkv: float32 [2, 384, 1152], P(None, 'fsdp')
- grad_qv_bias: float32 [2, 768], P(None, 'fsdp')
- grad_w_out: float32 [2, 384, 384], P(None, 'fsdp')
- grad_b_out: float32 [2, 384], P(None, 'fsdp')
- grad_w_up: float32 [2, 384, 1536], P(None, 'fsdp')
- grad_b_up: float32 [2, 1536], P(None, 'fsdp')
- grad_w_down: float32 [2, 1536, 384], P(None, 'fsdp')
- grad_b_down: float32 [2, 384], P(None, 'fsdp')
The draws below stay inside these ranges and needn't reach their ends.
All inputs are finite; a program needn't handle non-finite values.
Results may differ from the reference program's by a relative error of at most 0.029.
The reference program's roundings to bfloat16 on the way count: a program that leaves them out, or rounds other values in their place, can miss the bound.
Values may be sent and summed in bfloat16 or wider, within the bound.
No kernel may reach another device: no remote copies, remote signals or barrier semaphores. Data moves between devices by JAX's collectives and lax.ppermute only.
A program may use at most 320 MiB of HBM per device.

```python
import jax
import jax.numpy as jnp
from jax import lax

D = 384
FF = 1536
TOK = 256
LAYERS = 2
LATENTS = 256


def strengthened(values, key, source, target, shards_of, factor):
    owner, partner = [(jnp.arange(values.shape[axis_at]) // (values.shape[axis_at] // shards_of)).reshape([-1 if axis == axis_at else 1 for axis in range(values.ndim)]) for axis_at in (source, target)]
    chosen = jax.random.permutation(key, shards_of)[partner]
    strong = (owner == chosen) | (owner == (partner + shards_of // 2) % shards_of)
    return jnp.where(strong, factor * values, values)


def steps_of(own_key, extent, shards, smallest, high):
    factor_of, own = 1.0, jax.random.fold_in(own_key, 6)
    for position, blocks in shards:
        draws = jnp.exp(jax.random.uniform(jax.random.fold_in(own, position), (blocks,), jnp.float32, smallest / len(shards), high / len(shards)))
        factor_of = factor_of * jnp.repeat(draws, extent[position] // blocks).reshape([-1 if axis == position else 1 for axis in range(len(extent))])
    return factor_of


def normal_values(own_key, extent, deviation, reach, split=(), held_as=jnp.bfloat16):
    gain = steps_of(own_key, extent, split, -0.22, 0.18) if split else 1.0
    entries = jax.random.normal(own_key, extent, jnp.float32) * deviation * gain
    return jnp.minimum(jnp.maximum(entries, -reach), reach).astype(held_as)


def heavy_noise(own_key, dims, deviation, reach, shards, heavy, kind=jnp.bfloat16):
    array = deviation * jax.random.normal(own_key, dims, jnp.float32)
    if shards:
        array = array * steps_of(own_key, dims, shards, -0.22, 0.18)
    return jnp.clip(strengthened(array, jax.random.fold_in(own_key, 3), *heavy), -reach, reach).astype(kind)


def setup_inputs(seed: int = 0) -> dict:
    arg_keys = jax.random.split(jax.random.key(seed), 14)
    return {
        "latents": heavy_noise(arg_keys[0], (LATENTS, TOK, D), 1.0, 6.0, ((0, 32),), (0, 2, 32, 2.75), jnp.float32),
        "condition": heavy_noise(arg_keys[1], (LATENTS, D), 1.0, 6.0, ((0, 32),), (0, 1, 32, 2.75), jnp.float32),
        "cotangent": normal_values(arg_keys[2], (LATENTS, TOK, D), 1.0, 6.0, ((0, 32),), jnp.float32),
        "w_ada": normal_values(arg_keys[3], (LAYERS, D, 6 * D), D ** -0.5, 0.3125, ((1, 8),)),
        "b_ada": normal_values(arg_keys[4], (LAYERS, 6 * D), 0.5, 3.0, ((1, 8),)),
        "w_qkv": normal_values(arg_keys[5], (LAYERS, D, 3 * D), D ** -0.5, 0.3125, ((1, 8),)),
        "qv_bias": normal_values(arg_keys[6], (LAYERS, 2 * D), 0.5, 3.0, ((1, 8),)),
        "w_out": normal_values(arg_keys[7], (LAYERS, D, D), (D // 16) ** -0.5, 1.25, ((1, 8),)),
        "b_out": normal_values(arg_keys[8], (LAYERS, D), 0.5, 3.0, ((1, 8),)),
        "w_up": normal_values(arg_keys[9], (LAYERS, D, FF), D ** -0.5, 0.3125, ((1, 8),)),
        "b_up": normal_values(arg_keys[10], (LAYERS, FF), 0.5, 3.0, ((1, 8),)),
        "w_down": normal_values(arg_keys[11], (LAYERS, FF, D), FF ** -0.5, 0.15625, ((1, 8),)),
        "b_down": normal_values(arg_keys[12], (LAYERS, D), 0.5, 3.0, ((1, 8),)),
    }


GELU_C = 0.7978845608028654
GELU_A = 0.044715
EPS = 1e-06

def pair_product(form, left, right):
    return jnp.einsum(form, left.astype(jnp.float32), right.astype(jnp.float32), precision=lax.Precision.HIGHEST)

def matmul(inputs, weight):
    flattened = inputs.reshape(-1, inputs.shape[-1])
    result = jnp.dot(flattened, weight, preferred_element_type=jnp.float32)
    return result.reshape(inputs.shape[:-1] + (weight.shape[-1],))

def matmul_back(grads, weight):
    flattened = grads.reshape(-1, grads.shape[-1])
    result = lax.dot_general(flattened, weight, (((1,), (1,)), ((), ())), preferred_element_type=jnp.float32)
    return result.reshape(grads.shape[:-1] + (weight.shape[0],))

def outer_sum(left, right):
    return lax.dot_general(left.reshape(-1, left.shape[-1]), right.reshape(-1, right.shape[-1]), (((0,), (0,)), ((), ())), preferred_element_type=jnp.float32)

def norm_rows(stream):
    centered = stream - lax.optimization_barrier(jnp.mean(stream, axis=-1, keepdims=True))
    inverse = lax.rsqrt(lax.optimization_barrier(jnp.mean(centered * centered, axis=-1, keepdims=True)) + EPS)
    return (centered * inverse, inverse)

def norm_back(grad_normed, normed, inverse):
    return inverse * (grad_normed - lax.optimization_barrier(jnp.mean(grad_normed, axis=-1, keepdims=True)) - normed * lax.optimization_barrier(jnp.mean(grad_normed * normed, axis=-1, keepdims=True)))

def gelu_parts(pre_act):
    tanh_part = jnp.tanh(GELU_C * (pre_act + GELU_A * pre_act * pre_act * pre_act))
    value_part = 0.5 * pre_act * (1.0 + tanh_part)
    slope_part = 0.5 * (1.0 + tanh_part) + 0.5 * pre_act * (1.0 - tanh_part * tanh_part) * GELU_C * (1.0 + 3.0 * GELU_A * pre_act * pre_act)
    return (value_part, slope_part)

def forward_pieces(stream, cond_rows, params):
    w_ada, b_ada, w_qkv, qv_bias, w_out, b_out, w_up, b_up, w_down, b_down = params
    model_width = stream.shape[-1]
    head_count = model_width // 64
    silu_cond = jax.nn.silu(cond_rows).astype(jnp.bfloat16)
    modulation = jnp.dot(silu_cond, w_ada, preferred_element_type=jnp.float32) + b_ada.astype(jnp.float32)
    pieces = [modulation[:, None, i * model_width:(i + 1) * model_width] for i in range(6)]
    shift1, scale1, gate1, shift2, scale2, gate2 = pieces
    normed1, inverse1 = norm_rows(stream)
    attn_in = (normed1 * (1.0 + scale1) + shift1).astype(jnp.bfloat16)
    bias_query = qv_bias[:model_width].astype(jnp.float32)
    bias_value = qv_bias[model_width:].astype(jnp.float32)
    full_bias = jnp.concatenate([bias_query, jnp.zeros_like(bias_query), bias_value])
    projected = (matmul(attn_in, w_qkv) + full_bias).astype(jnp.bfloat16)
    head_shape = stream.shape[:2] + (head_count, 64)
    query = projected[..., :model_width].reshape(head_shape)
    key_heads = projected[..., model_width:2 * model_width].reshape(head_shape)
    value_heads = projected[..., 2 * model_width:].reshape(head_shape)
    scores = pair_product('bqhe,bkhe->bhqk', query, key_heads) * 0.125
    log_total = jax.nn.logsumexp(scores, axis=-1, keepdims=True)
    attention = jnp.exp(scores - log_total)
    attention_b = attention.astype(jnp.bfloat16)
    attended = pair_product('bhqk,bkhe->bqhe', attention_b, value_heads).astype(jnp.bfloat16).reshape(stream.shape)
    branch = matmul(attended, w_out) + b_out.astype(jnp.float32)
    middle = stream + gate1 * branch
    normed2, inverse2 = norm_rows(middle)
    mlp_in = (normed2 * (1.0 + scale2) + shift2).astype(jnp.bfloat16)
    hidden_pre = matmul(mlp_in, w_up) + b_up.astype(jnp.float32)
    activated_f, slope = gelu_parts(hidden_pre)
    activated = activated_f.astype(jnp.bfloat16)
    mlp_out = matmul(activated, w_down) + b_down.astype(jnp.float32)
    result = middle + gate2 * mlp_out
    saved = (silu_cond, pieces, normed1, inverse1, attn_in, query, key_heads, value_heads, attention, attention_b, attended, branch, normed2, inverse2, mlp_in, slope, activated, mlp_out)
    return (result, saved)

def layer_forward(stream, cond_rows, params):
    return forward_pieces(stream, cond_rows, params)[0]

def layer_grads(stream, cond_rows, params, grad_result):
    w_ada, b_ada, w_qkv, qv_bias, w_out, b_out, w_up, b_up, w_down, b_down = params
    result, saved = forward_pieces(stream, cond_rows, params)
    silu_cond, pieces, normed1, inverse1, attn_in, query, key_heads, value_heads, attention, attention_b, attended, branch, normed2, inverse2, mlp_in, slope, activated, mlp_out = saved
    shift1, scale1, gate1, shift2, scale2, gate2 = pieces
    grad_z = gate2 * grad_result
    grad_z_b = grad_z.astype(jnp.bfloat16)
    grad_gate2 = lax.optimization_barrier(jnp.sum(grad_result * mlp_out, axis=1))
    grad_b_down = lax.optimization_barrier(jnp.sum(grad_z, axis=(0, 1)))
    grad_w_down = outer_sum(activated, grad_z_b)
    grad_pre = matmul_back(grad_z_b, w_down) * slope
    grad_pre_b = grad_pre.astype(jnp.bfloat16)
    grad_b_up = lax.optimization_barrier(jnp.sum(grad_pre, axis=(0, 1)))
    grad_w_up = outer_sum(mlp_in, grad_pre_b)
    grad_mlp_in = matmul_back(grad_pre_b, w_up)
    grad_scale2 = lax.optimization_barrier(jnp.sum(grad_mlp_in * normed2, axis=1))
    grad_shift2 = lax.optimization_barrier(jnp.sum(grad_mlp_in, axis=1))
    grad_middle = grad_result + norm_back(grad_mlp_in * (1.0 + scale2), normed2, inverse2)
    grad_branch = gate1 * grad_middle
    grad_branch_b = grad_branch.astype(jnp.bfloat16)
    grad_gate1 = lax.optimization_barrier(jnp.sum(grad_middle * branch, axis=1))
    grad_b_out = lax.optimization_barrier(jnp.sum(grad_branch, axis=(0, 1)))
    grad_w_out = outer_sum(attended, grad_branch_b)
    grad_attended = matmul_back(grad_branch_b, w_out).astype(jnp.bfloat16).reshape(query.shape)
    grad_value = pair_product('bhqk,bqhe->bkhe', attention_b, grad_attended)
    grad_probs = pair_product('bqhe,bkhe->bhqk', grad_attended, value_heads)
    row_dot = lax.optimization_barrier(jnp.sum(attention * grad_probs, axis=-1, keepdims=True))
    grad_scores = (attention * (grad_probs - row_dot) * 0.125).astype(jnp.bfloat16)
    grad_query = pair_product('bhqk,bkhe->bqhe', grad_scores, key_heads)
    grad_key = pair_product('bhqk,bqhe->bkhe', grad_scores, query)
    flat_shape = stream.shape
    grad_proj = jnp.concatenate([grad_query.reshape(flat_shape), grad_key.reshape(flat_shape), grad_value.reshape(flat_shape)], axis=-1)
    grad_proj_b = grad_proj.astype(jnp.bfloat16)
    grad_qv_bias = jnp.concatenate([lax.optimization_barrier(jnp.sum(grad_query.reshape(flat_shape), axis=(0, 1))), lax.optimization_barrier(jnp.sum(grad_value.reshape(flat_shape), axis=(0, 1)))])
    grad_w_qkv = outer_sum(attn_in, grad_proj_b)
    grad_attn_in = matmul_back(grad_proj_b, w_qkv)
    grad_scale1 = lax.optimization_barrier(jnp.sum(grad_attn_in * normed1, axis=1))
    grad_shift1 = lax.optimization_barrier(jnp.sum(grad_attn_in, axis=1))
    grad_stream = grad_middle + norm_back(grad_attn_in * (1.0 + scale1), normed1, inverse1)
    grad_mod = jnp.concatenate([grad_shift1, grad_scale1, grad_gate1, grad_shift2, grad_scale2, grad_gate2], axis=-1)
    grad_w_ada = jnp.dot(silu_cond.astype(jnp.float32).T, grad_mod, precision=lax.Precision.HIGHEST)
    grad_b_ada = lax.optimization_barrier(jnp.sum(grad_mod, axis=0))
    grad_silu = jnp.dot(grad_mod, w_ada.astype(jnp.float32).T, precision=lax.Precision.HIGHEST)
    sigmoid_c = jax.nn.sigmoid(cond_rows)
    grad_cond = grad_silu * sigmoid_c * (1.0 + cond_rows * (1.0 - sigmoid_c))
    gradients = (grad_w_ada, grad_b_ada, grad_w_qkv, grad_qv_bias, grad_w_out, grad_b_out, grad_w_up, grad_b_up, grad_w_down, grad_b_down)
    return (grad_stream, grad_cond, gradients)

def reference(latents, condition, cotangent, w_ada, b_ada, w_qkv, qv_bias, w_out, b_out, w_up, b_up, w_down, b_down):
    stacked = (w_ada, b_ada, w_qkv, qv_bias, w_out, b_out, w_up, b_up, w_down, b_down)
    group_size = 16
    group_count = LATENTS // group_size

    def regroup(array_item):
        return array_item.reshape((group_count, group_size) + array_item.shape[1:])
    empty_sums = tuple((jnp.zeros(weight.shape, jnp.float32) for weight in stacked))

    def group_step(totals, group_data):
        stream, cond_rows, grad_out = group_data
        inputs = []
        for layer_index in range(LAYERS):
            params = tuple((weight[layer_index] for weight in stacked))
            inputs.append(stream)
            stream = layer_forward(stream, cond_rows, params)
        grad_stream = grad_out
        grad_cond = jnp.zeros(cond_rows.shape, jnp.float32)
        per_layer = [None] * LAYERS
        for layer_index in reversed(range(LAYERS)):
            params = tuple((weight[layer_index] for weight in stacked))
            grad_stream, cond_part, gradients = layer_grads(inputs[layer_index], cond_rows, params, grad_stream)
            grad_cond = grad_cond + cond_part
            per_layer[layer_index] = gradients
        new_totals = tuple((totals[i] + jnp.stack([per_layer[j][i] for j in range(LAYERS)]) for i in range(10)))
        return (new_totals, (stream, grad_stream, grad_cond))
    totals, (outputs, grad_lat, grad_cond) = lax.scan(group_step, empty_sums, (regroup(latents), regroup(condition), regroup(cotangent)))
    return (outputs.reshape(latents.shape), grad_lat.reshape(latents.shape), grad_cond.reshape(condition.shape), totals[0], totals[1], totals[2], totals[3], totals[4], totals[5], totals[6], totals[7], totals[8], totals[9])
```

```python
import functools

import jax
import jax.numpy as jnp
from jax import lax
from jax.experimental import pallas as pl
from jax.experimental.pallas import tpu as pltpu
from jax.sharding import PartitionSpec as P

GELU_C = 0.7978845608028654
GELU_A = 0.044715
EPS = 1e-06
HEAD = 64
LANES = 128
F32 = jnp.float32
BF16 = jnp.bfloat16


def dot(left, right, contract=((1,), (0,))):
    return lax.dot_general(left, right, (contract, ((), ())), preferred_element_type=F32)


def dot_t(left, right):
    return dot(left, right, ((1,), (1,)))


def row_mean(x):
    return jnp.sum(x, axis=-1, keepdims=True) * (1.0 / x.shape[-1])


def norm_rows(x):
    centered = x - row_mean(x)
    inverse = lax.rsqrt(row_mean(centered * centered) + EPS)
    return centered * inverse, inverse


def norm_back(grad, normed, inverse):
    return inverse * (grad - row_mean(grad) - normed * row_mean(grad * normed))


def col_sum(x):
    return jnp.sum(x, axis=0, keepdims=True)


def split_hi_lo(x):
    hi = x.astype(BF16)
    lo = (x - hi.astype(F32)).astype(BF16)
    return jnp.concatenate([hi, lo], axis=0)


def my_place():
    return lax.axis_index("fsdp"), lax.axis_index("rep") & 1


def weight_copies(pieces, rels, plan, sems):
    me, core = my_place()
    copies = []
    at = 0
    for piece, (rel_even, rel_odd, only) in zip(pieces, rels):
        rows = piece.shape[0]
        owner = me ^ jnp.where(core == 0, rel_even, rel_odd)
        for scratch, first, width, parts in plan:
            for part in range(parts):
                start = pl.multiple_of((owner * parts + part) * rows, rows)
                copies.append(
                    (
                        only,
                        pltpu.make_async_copy(
                            piece.at[:, pl.ds(first + part * width, width)],
                            scratch.at[pl.ds(start, rows), :],
                            sems.at[at],
                        ),
                    )
                )
                at += 1
    return copies


def on_place(only, action):
    if only is None:
        action()
    else:
        _, core = my_place()
        pl.when(core == only)(action)


class Columns:
    def __init__(self, rows, width, hidden):
        self.rows, self.width, self.hidden = rows, width, hidden
        self.parts = hidden // width
        w = width
        self.attn = {"ada": (0, 3 * w), "qkv": (3 * w, 3 * w), "out": (6 * w, w)}
        self.mlp = {"ada": (0, 3 * w), "up": (3 * w, hidden), "down": (3 * w + hidden, hidden)}
        self.attn_end = 7 * w
        self.mlp_end = 3 * w + 2 * hidden
        sizes = (6 * w, 3 * w, w, hidden, w)
        names = ("ada", "qkv", "out", "up", "down")
        self.bias, at = {}, 0
        for name, size in zip(names, sizes):
            self.bias[name] = (at, size)
            at += size
        self.bias_size = at
        self.attn_sums = {"ada": (0, 3 * w), "qv": (3 * w, 2 * w), "out": (5 * w, w)}
        self.mlp_sums = {"ada": (0, 3 * w), "up": (3 * w, hidden), "down": (3 * w + hidden, w)}
        self.attn_grad = self.even(self.attn_end + self.tiles(6 * w) * LANES)
        self.mlp_grad = self.even(self.mlp_end + self.tiles(4 * w + hidden) * LANES)

    def tiles(self, size):
        return -(-size // (LANES * self.rows))

    def even(self, columns):
        return -(-columns // (2 * LANES)) * 2 * LANES

    def attn_plan(self, base=0):
        w = self.width
        return [
            ((w, 3 * w), base + self.attn["ada"][0], 3 * w, 1),
            ((w, 3 * w), base + self.attn["qkv"][0], 3 * w, 1),
            ((w, w), base + self.attn["out"][0], w, 1),
        ]

    def mlp_plan(self, base=0):
        w, hidden = self.width, self.hidden
        return [
            ((w, 3 * w), base + self.mlp["ada"][0], 3 * w, 1),
            ((w, hidden), base + self.mlp["up"][0], hidden, 1),
            ((hidden, w), base + self.mlp["down"][0], w, self.parts),
        ]


def put_grad(refs, owner, first, value):
    me, _ = my_place()
    half_width = refs[0].shape[-1]
    width = value.shape[-1]
    for half in range(2):
        lo, hi = max(first, half * half_width), min(first + width, (half + 1) * half_width)
        if lo < hi:
            refs[half][owner ^ me, :, lo - half * half_width : hi - half * half_width] = value[
                :, lo - first : hi - first
            ].astype(BF16)


def put_sums(refs, tile_ref, rows, first):
    owners = refs[0].shape[0]
    for block in range(tile_ref.shape[0] // rows):
        tile = tile_ref[block * rows : (block + 1) * rows, :]
        for owner in range(owners):
            put_grad(refs, owner, first + block * LANES, tile)


def fill_sums(tile_ref, sums):
    tile_ref[...] = jnp.zeros_like(tile_ref)
    at = 0
    for row in sums:
        for lo in range(0, row.shape[-1], LANES):
            tile_ref[at : at + 1, :] = row[:, lo : lo + LANES]
            at += 1


def by_core(keep_ref, away_ref, write):
    _, core = my_place()

    @pl.when(core == 0)
    def _():
        write((keep_ref, away_ref))

    @pl.when(core != 0)
    def _():
        write((away_ref, keep_ref))


def lane_masks(tokens):
    lane = lax.broadcasted_iota(jnp.int32, (tokens, LANES), 1)
    return lane < HEAD, lane >= HEAD


def attn_fwd_body(args, weights, outs, per_step):
    s_ref, b_ada, b_qkv, b_out, h_ref = args
    w_ada, w_qkv, w_out = weights
    mod_ref, h2_ref, qkv_ref, p_ref, o_ref, y_ref = outs
    step = pl.program_id(0)
    width = h_ref.shape[-1]
    tokens = h_ref.shape[1]
    masks = lane_masks(tokens)
    zero = jnp.zeros((), BF16)

    @pl.when(step == 0)
    def _():
        mod_ref[...] = dot(s_ref[...], w_ada[...]) + b_ada

    for at in range(per_step):
        mod = mod_ref[pl.ds(step * per_step + at, 1), :]
        shift, scale, gate = (mod[:, i * width : (i + 1) * width] for i in range(3))
        h = h_ref[at]
        normed, _ = norm_rows(h)
        a = (normed * (1.0 + scale) + shift).astype(BF16)
        qkv = dot(a, w_qkv[...]) + b_qkv
        qkv_b = qkv.astype(BF16)
        qkv_ref[at] = qkv_b
        attended = []
        for pair in range(width // LANES):
            lo = pair * LANES
            query = (qkv[:, lo : lo + LANES] * 0.125).astype(BF16)
            key = qkv_b[:, width + lo : width + lo + LANES]
            value = qkv_b[:, 2 * width + lo : 2 * width + lo + LANES]
            total = None
            for e in range(2):
                scores = dot_t(query, jnp.where(masks[e], key, zero))
                top = jnp.max(scores, axis=-1, keepdims=True)
                grown = jnp.exp(scores - top)
                p = grown * (1.0 / jnp.sum(grown, axis=-1, keepdims=True))
                p_ref[at, 2 * pair + e] = p
                part = dot(p.astype(BF16), jnp.where(masks[e], value, zero))
                total = part if total is None else total + part
            attended.append(total.astype(BF16))
        o = jnp.concatenate(attended, axis=1)
        o_ref[at] = o
        y = dot(o, w_out[...]) + b_out
        y_ref[at] = y
        h2_ref[at] = h + gate * y


def mlp_fwd_body(args, weights, outs, per_step, chunk):
    s_ref, b_ada, b_up, b_down, h2_ref = args
    w_ada, w_up, w_down = weights
    mod_ref, h3_ref, m_ref, g_ref, slope_ref, z_ref = outs
    step = pl.program_id(0)
    width = h2_ref.shape[-1]
    hidden = w_up.shape[-1]

    @pl.when(step == 0)
    def _():
        mod_ref[...] = dot(s_ref[...], w_ada[...]) + b_ada

    for at in range(per_step):
        mod = mod_ref[pl.ds(step * per_step + at, 1), :]
        shift, scale, gate = (mod[:, i * width : (i + 1) * width] for i in range(3))
        h2 = h2_ref[at]
        normed, _ = norm_rows(h2)
        m = (normed * (1.0 + scale) + shift).astype(BF16)
        m_ref[at] = m
        z = None
        for first in range(0, hidden, chunk):
            span = slice(first, first + chunk)
            u = dot(m, w_up[:, span]) + b_up[:, span]
            square = u * u
            t = jnp.tanh(GELU_C * (u + GELU_A * (square * u)))
            half = 0.5 * (1.0 + t)
            g = (u * half).astype(BF16)
            slope_ref[at, :, span] = half + (0.5 * GELU_C) * u * (1.0 - t * t) * (
                1.0 + (3.0 * GELU_A) * square
            )
            g_ref[at, :, span] = g
            part = dot(g, w_down[span, :])
            z = part if z is None else z + part
        z = z + b_down
        z_ref[at] = z
        h3_ref[at] = h2 + gate * z


def mlp_bwd_body(args, weights, outs, accs, per_step, chunk, cols):
    s_ref, mod_ref, h2_ref, dh3_ref, m_ref, g_ref, slope_ref, z_ref = args
    w_ada, w_up, w_down = weights
    dcond_ref, keep_ref, away_ref, dh2_ref = outs
    acc_up, acc_down, dmod_ref, bias_ref, tile_ref, ada_ref, down_ref = accs
    step = pl.program_id(0)
    last = pl.num_programs(0) - 1
    width = h2_ref.shape[-1]
    hidden = w_up.shape[-1]

    @pl.when(step == 0)
    def _():
        acc_up[...] = jnp.zeros_like(acc_up)
        acc_down[...] = jnp.zeros_like(acc_down)
        bias_ref[...] = jnp.zeros_like(bias_ref)

    for at in range(per_step):
        row = step * per_step + at
        mod = mod_ref[pl.ds(row, 1), :]
        scale, gate = mod[:, width : 2 * width], mod[:, 2 * width : 3 * width]
        dh3 = dh3_ref[at]
        dz = gate * dh3
        dzb = dz.astype(BF16)
        dzb_t = dzb.T
        m_t = m_ref[at].T
        bias_ref[:, hidden : hidden + width] += col_sum(dz)
        dm = None
        for first in range(0, hidden, chunk):
            span = slice(first, first + chunk)
            du = dot_t(dzb, w_down[span, :]) * slope_ref[at, :, span]
            dub = du.astype(BF16)
            bias_ref[:, span] += col_sum(du)
            acc_down[:, span] += dot(dzb_t, g_ref[at, :, span])
            acc_up[:, span] += dot(m_t, dub)
            part = dot_t(dub, w_up[:, span])
            dm = part if dm is None else dm + part
        normed, inverse = norm_rows(h2_ref[at])
        dmod_ref[pl.ds(row, 1), :] = jnp.concatenate(
            [col_sum(dm), col_sum(dm * normed), col_sum(dh3 * z_ref[at])], axis=1
        )
        dh2_ref[at] = dh3 + norm_back(dm * (1.0 + scale), normed, inverse)

    @pl.when(step == last)
    def _():
        ada = ada_tail(s_ref, w_ada, dmod_ref, dcond_ref)
        ada_ref[...] = ada
        down_ref[...] = acc_down[...].T
        fill_sums(tile_ref, [col_sum(dmod_ref[...]), bias_ref[...]])
        rows = cols.rows

        def write(refs):
            for owner in range(refs[0].shape[0]):
                mine = slice(owner * rows, (owner + 1) * rows)
                put_grad(refs, owner, 0, ada_ref[mine, :])
                put_grad(refs, owner, cols.mlp["up"][0], acc_up[mine, :])
                for part in range(cols.parts):
                    first = (owner * cols.parts + part) * rows
                    put_grad(
                        refs,
                        owner,
                        cols.mlp["down"][0] + part * width,
                        down_ref[first : first + rows, :],
                    )
            put_sums(refs, tile_ref, rows, cols.mlp_end)

        by_core(keep_ref, away_ref, write)


def ada_tail(s_ref, w_ada, dmod_ref, dcond_ref):
    parts = split_hi_lo(dmod_ref[...])
    rows = dmod_ref.shape[0]
    both = dot_t(parts, w_ada[...])
    dcond_ref[...] = both[:rows] + both[rows:]
    s = s_ref[...]
    return dot(jnp.concatenate([s, s], axis=0), parts, ((0,), (0,)))


def attn_bwd_body(args, weights, outs, accs, per_step, cols):
    s_ref, mod_ref, h_ref, dh2_ref, qkv_ref, p_ref, o_ref, y_ref = args
    w_ada, w_qkv, w_out = weights
    dcond_ref, keep_ref, away_ref, dh_ref = outs
    acc_qkv, acc_out, dqkv_ref, dmod_ref, bias_ref, tile_ref, ada_ref = accs
    step = pl.program_id(0)
    last = pl.num_programs(0) - 1
    width = h_ref.shape[-1]
    tokens = h_ref.shape[1]
    masks = lane_masks(tokens)
    zero = jnp.zeros((), BF16)

    @pl.when(step == 0)
    def _():
        acc_qkv[...] = jnp.zeros_like(acc_qkv)
        acc_out[...] = jnp.zeros_like(acc_out)
        bias_ref[...] = jnp.zeros_like(bias_ref)

    for at in range(per_step):
        row = step * per_step + at
        mod = mod_ref[pl.ds(row, 1), :]
        shift, scale, gate = (mod[:, i * width : (i + 1) * width] for i in range(3))
        dh2 = dh2_ref[at]
        dy = gate * dh2
        dyb = dy.astype(BF16)
        bias_ref[:, 2 * width : 3 * width] += col_sum(dy)
        acc_out[...] += dot(o_ref[at].T, dyb)
        do = dot_t(dyb, w_out[...]).astype(BF16)
        do_t = do.T
        query_t = qkv_ref[at, :, :width].T
        dk_t, dv_t = [], []
        for pair in range(width // LANES):
            lo = pair * LANES
            key = qkv_ref[at, :, width + lo : width + lo + LANES]
            value = qkv_ref[at, :, 2 * width + lo : 2 * width + lo + LANES]
            do_pair = do[:, lo : lo + LANES]
            dq = None
            for e in range(2):
                head = 2 * pair + e
                rows = slice(head * HEAD, (head + 1) * HEAD)
                p = p_ref[at, head]
                dp = dot_t(do_pair, jnp.where(masks[e], value, zero))
                inner = jnp.sum(p * dp, axis=-1, keepdims=True)
                ds = (p * (dp - inner) * 0.125).astype(BF16)
                dv_t.append(dot(do_t[rows], p.astype(BF16)))
                dk_t.append(dot(query_t[rows], ds))
                part = dot(ds, jnp.where(masks[e], key, zero))
                dq = part if dq is None else dq + part
            bias_ref[:, lo : lo + LANES] += col_sum(dq)
            dqkv_ref[:, lo : lo + LANES] = dq.astype(BF16)
        dv = jnp.concatenate(dv_t, axis=0).T
        bias_ref[:, width : 2 * width] += col_sum(dv)
        dqkv_ref[:, width : 2 * width] = jnp.concatenate(dk_t, axis=0).T.astype(BF16)
        dqkv_ref[:, 2 * width :] = dv.astype(BF16)
        normed, inverse = norm_rows(h_ref[at])
        a = (normed * (1.0 + scale) + shift).astype(BF16)
        acc_qkv[...] += dot(a.T, dqkv_ref[...])
        da = dot_t(dqkv_ref[...], w_qkv[...])
        dmod_ref[pl.ds(row, 1), :] = jnp.concatenate(
            [col_sum(da), col_sum(da * normed), col_sum(dh2 * y_ref[at])], axis=1
        )
        dh_ref[at] = dh2 + norm_back(da * (1.0 + scale), normed, inverse)

    @pl.when(step == last)
    def _():
        ada = ada_tail(s_ref, w_ada, dmod_ref, dcond_ref)
        ada_ref[...] = ada
        fill_sums(tile_ref, [col_sum(dmod_ref[...]), bias_ref[...]])
        rows = cols.rows

        def write(refs):
            for owner in range(refs[0].shape[0]):
                mine = slice(owner * rows, (owner + 1) * rows)
                put_grad(refs, owner, 0, ada_ref[mine, :])
                put_grad(refs, owner, cols.attn["qkv"][0], acc_qkv[mine, :])
                put_grad(refs, owner, cols.attn["out"][0], acc_out[mine, :])
            put_sums(refs, tile_ref, rows, cols.attn_end)

        by_core(keep_ref, away_ref, write)


def per_latent(shape, per_step):
    rest = shape[1:]
    return pl.BlockSpec((per_step,) + rest, lambda b: (b,) + (0,) * len(rest))


def whole(shape):
    return pl.BlockSpec(shape, lambda b: (0,) * len(shape))


def sds(shape, dtype=F32):
    return jax.ShapeDtypeStruct(tuple(shape), dtype)


def params(steps=True):
    return pltpu.CompilerParams(
        dimension_semantics=("arbitrary",) if steps else None, vmem_limit_bytes=60 * 2**20
    )


def estimate(micros):
    return pl.CostEstimate(flops=int(micros * 1.0e9), bytes_accessed=int(micros * 1.0e6), transcendentals=0)


def run(body, constants, streams, gathered, plan, out_constants, out_streams, scratch, per_step, name, micros):
    latents = streams[0].shape[0]
    pieces, rels = gathered
    direct = rels is None
    n_in = len(constants) + len(streams)
    n_out = len(out_streams) + len(out_constants)
    copies = 0 if direct else len(pieces) * sum(parts for _, _, _, parts in plan)

    def kernel(*refs):
        ins, rest = refs[:n_in], refs[n_in:]
        got, rest = rest[: len(pieces)], rest[len(pieces) :]
        outs, rest = rest[:n_out], rest[n_out:]
        if direct:
            weights, accs = got, rest
        else:
            weights, sems, accs = rest[: len(plan)], rest[len(plan)], rest[len(plan) + 1 :]

            @pl.when(pl.program_id(0) == 0)
            def _():
                started = weight_copies(
                    got, rels, [(w,) + tuple(p[1:]) for w, p in zip(weights, plan)], sems
                )
                for only, copy in started:
                    on_place(only, copy.start)
                for only, copy in started:
                    on_place(only, copy.wait)

        body(ins, weights, outs, accs)

    if direct:
        piece_specs = [whole(p.shape) for p in pieces]
        extra = []
    else:
        piece_specs = [pl.BlockSpec(memory_space=pl.ANY)] * len(pieces)
        extra = [pltpu.VMEM(shape, BF16) for shape, _, _, _ in plan]
        extra.append(pltpu.SemaphoreType.DMA((copies,)))
    return pl.pallas_call(
        kernel,
        grid=(latents // per_step,),
        in_specs=[whole(c.shape) for c in constants]
        + [per_latent(x.shape, per_step) for x in streams]
        + piece_specs,
        out_specs=[whole(x.shape) for x in out_constants]
        + [per_latent(x.shape, per_step) for x in out_streams],
        out_shape=list(out_constants) + list(out_streams),
        scratch_shapes=extra + list(scratch),
        compiler_params=params(),
        cost_estimate=estimate(micros),
        name=name,
    )(*constants, *streams, *pieces)


def layer_bias(bias_ref, cols, layer, name, part=None):
    first, size = cols.bias[name]
    first += layer * cols.bias_size
    if part is not None:
        size //= 2
        first += part * size
    return bias_ref[:, first : first + size]


def attn_fwd(h, s, bias, gathered, plan, cols, layer, per_step=1):
    n, tokens, width = h.shape

    def body(ins, weights, outs, _):
        s_ref, bias_ref, h_ref = ins
        biases = (
            layer_bias(bias_ref, cols, layer, "ada", 0),
            layer_bias(bias_ref, cols, layer, "qkv"),
            layer_bias(bias_ref, cols, layer, "out"),
        )
        attn_fwd_body((s_ref,) + biases + (h_ref,), weights, outs, per_step)

    return run(
        body,
        [s, bias],
        [h],
        gathered,
        plan,
        [sds((n, 3 * width))],
        [
            sds(h.shape),
            sds((n, tokens, 3 * width), BF16),
            sds((n, width // HEAD, tokens, tokens)),
            sds(h.shape, BF16),
            sds(h.shape),
        ],
        [],
        per_step,
        "attn_fwd",
        20,
    )


def mlp_fwd(h2, s, bias, gathered, plan, cols, layer, per_step=1, chunk=256):
    n, tokens, width = h2.shape
    hidden = cols.hidden

    def body(ins, weights, outs, _):
        s_ref, bias_ref, h2_ref = ins
        biases = (
            layer_bias(bias_ref, cols, layer, "ada", 1),
            layer_bias(bias_ref, cols, layer, "up"),
            layer_bias(bias_ref, cols, layer, "down"),
        )
        mlp_fwd_body((s_ref,) + biases + (h2_ref,), weights, outs, per_step, chunk)

    return run(
        body,
        [s, bias],
        [h2],
        gathered,
        plan,
        [sds((n, 3 * width))],
        [
            sds(h2.shape),
            sds(h2.shape, BF16),
            sds((n, tokens, hidden), BF16),
            sds((n, tokens, hidden)),
            sds(h2.shape),
        ],
        [],
        per_step,
        "mlp_fwd",
        22,
    )


def mlp_bwd(s, mod, h2, dh3, m, g, slope, z, gathered, plan, cols, owners, per_step=1, chunk=256):
    n, tokens, width = h2.shape
    hidden = cols.hidden

    def body(ins, weights, outs, accs):
        mlp_bwd_body(ins, weights, outs, accs, per_step, chunk, cols)

    return run(
        body,
        [s, mod],
        [h2, dh3, m, g, slope, z],
        gathered,
        plan,
        [sds((n, width))] + [sds((owners, cols.rows, cols.mlp_grad // 2), BF16)] * 2,
        [sds(h2.shape)],
        [
            pltpu.VMEM((width, hidden), F32),
            pltpu.VMEM((width, hidden), F32),
            pltpu.VMEM((n, 3 * width), F32),
            pltpu.VMEM((1, hidden + width), F32),
            pltpu.VMEM((cols.tiles(4 * width + hidden) * cols.rows, LANES), F32),
            pltpu.VMEM((width, 3 * width), F32),
            pltpu.VMEM((hidden, width), F32),
        ],
        per_step,
        "mlp_bwd",
        24,
    )


def attn_bwd(s, mod, h, dh2, qkv, p, o, y, gathered, plan, cols, owners, per_step=1):
    n, tokens, width = h.shape

    def body(ins, weights, outs, accs):
        attn_bwd_body(ins, weights, outs, accs, per_step, cols)

    return run(
        body,
        [s, mod],
        [h, dh2, qkv, p, o, y],
        gathered,
        plan,
        [sds((n, width))] + [sds((owners, cols.rows, cols.attn_grad // 2), BF16)] * 2,
        [sds(h.shape)],
        [
            pltpu.VMEM((width, 3 * width), F32),
            pltpu.VMEM((width, width), F32),
            pltpu.VMEM((tokens, 3 * width), BF16),
            pltpu.VMEM((n, 3 * width), F32),
            pltpu.VMEM((1, 3 * width), F32),
            pltpu.VMEM((cols.tiles(6 * width) * cols.rows, LANES), F32),
            pltpu.VMEM((width, 3 * width), F32),
        ],
        per_step,
        "attn_bwd",
        28,
    )


def simple_call(kernel, args, outs, name, scratch=()):
    vmem = pl.BlockSpec(memory_space=pltpu.VMEM)
    return pl.pallas_call(
        kernel,
        in_specs=[vmem] * len(args),
        out_specs=[vmem] * len(outs),
        out_shape=list(outs),
        scratch_shapes=list(scratch),
        compiler_params=params(False),
        cost_estimate=estimate(1),
        name=name,
    )(*args)


def pack_shards(stacked, cols, owners, layers):
    rows, width, hidden = cols.rows, cols.width, cols.hidden
    tiles = cols.tiles(layers * cols.bias_size)
    names = ("ada", "qkv", "out", "up", "down")

    def kernel(w_ada, b_ada, w_qkv, qv_bias, w_out, b_out, w_up, b_up, w_down, b_down, *refs):
        outs, row_ref, tile_ref = refs[:-2], refs[-2], refs[-1]
        me, _ = my_place()
        for layer in range(layers):
            attn_ref = outs[0] if layer == 0 else outs[layer + 1]
            mlp_ref = outs[1] if layer == 0 else outs[layer + 1]
            base = 0 if layer == 0 else cols.attn_end
            attn_ref[:, : 3 * width] = w_ada[layer, :, : 3 * width]
            attn_ref[:, 3 * width : 6 * width] = w_qkv[layer]
            attn_ref[:, 6 * width : 7 * width] = w_out[layer]
            mlp_ref[:, base : base + 3 * width] = w_ada[layer, :, 3 * width :]
            first = base + 3 * width
            mlp_ref[:, first : first + hidden] = w_up[layer]
            first += hidden
            for part in range(cols.parts):
                mlp_ref[:, first + part * width : first + (part + 1) * width] = w_down[
                    layer, part * rows : (part + 1) * rows, :
                ]
        row_ref[...] = jnp.zeros_like(row_ref)
        for owner in range(owners):

            @pl.when(me == owner)
            def _():
                for layer in range(layers):
                    for name, ref in zip(names, (b_ada, qv_bias, b_out, b_up, b_down)):
                        size = ref.shape[-1]
                        at = layer * cols.bias_size + cols.bias[name][0] + owner * size
                        if name == "qkv" and 2 * owner >= owners:
                            at += width
                        row_ref[:, at : at + size] = ref[layer : layer + 1, :].astype(F32)

        tile_ref[...] = jnp.zeros_like(tile_ref)
        for at in range(layers * cols.bias_size // LANES):
            tile_ref[at : at + 1, :] = row_ref[:, at * LANES : (at + 1) * LANES]
        for tile in range(tiles):
            outs[0][:, cols.attn_end + tile * LANES : cols.attn_end + (tile + 1) * LANES] = tile_ref[
                tile * rows : (tile + 1) * rows, :
            ].astype(BF16)

    outs = [sds((rows, cols.attn_end + tiles * LANES), BF16), sds((rows, cols.mlp_end), BF16)]
    outs += [sds((rows, cols.attn_end + cols.mlp_end), BF16)] * (layers - 1)
    scratch = [pltpu.VMEM((1, layers * cols.bias_size), F32), pltpu.VMEM((tiles * rows, LANES), F32)]
    return simple_call(kernel, stacked, outs, "pack", scratch)


def sum_bias(tiles, cols, layers, only_of):
    rows = cols.rows

    def kernel(*refs):
        ins, out_ref, sum_ref = refs[:-2], refs[-2], refs[-1]
        _, core = my_place()
        total = None
        for ref, only in zip(ins, only_of):
            value = ref[...].astype(F32)
            if only is not None:
                value = jnp.where(core == only, value, 0.0)
            total = value if total is None else total + value
        for tile in range(total.shape[1] // LANES):
            sum_ref[tile * rows : (tile + 1) * rows, :] = total[:, tile * LANES : (tile + 1) * LANES]
        for at in range(layers * cols.bias_size // LANES):
            out_ref[:, at * LANES : (at + 1) * LANES] = sum_ref[at : at + 1, :]

    count = tiles[0].shape[1] // LANES
    (out,) = simple_call(
        kernel,
        tiles,
        [sds((1, layers * cols.bias_size))],
        "sum_bias",
        [pltpu.VMEM((count * rows, LANES), F32)],
    )
    return out


class Slice:
    def __init__(self, mesh):
        self.owners, self.reps = mesh.shape["fsdp"], mesh.shape["rep"]

    def send(self, x, rel_even=0, rel_odd=None, swap=0, only=None):
        rel_odd = rel_even if rel_odd is None else rel_odd
        pairs = []
        for f in range(self.owners):
            for r in range(self.reps):
                rel = rel_odd if r & 1 else rel_even
                if only is None or (r & 1) == only:
                    pairs.append((f * self.reps + r, (f ^ rel) * self.reps + (r ^ swap)))
        return lax.ppermute(x, ("fsdp", "rep"), pairs)


def can_share(slc, rows):
    return slc.owners == 8 and slc.reps % 2 == 0 and rows % 16 == 0


RELS = (
    (0, 0, None),
    (2, 4, None),
    (6, 1, None),
    (4, 2, None),
    (1, 6, None),
    (3, 5, None),
    (5, 3, None),
    (7, 7, 0),
    (7, 7, 1),
)


def gather(piece, slc):
    first, second = yield (slc.send(piece, 2, 4), slc.send(piece, 6, 1))
    first_x, second_x = slc.send(first, swap=1), slc.send(second, swap=1)
    third, fourth = slc.send(first, 1, 1), slc.send(second, 1, only=0)
    first_x, second_x, third, fourth = yield (first_x, second_x, third, fourth)
    third_x, fourth_x = yield (slc.send(third, swap=1), slc.send(fourth, swap=1, only=0))
    return (piece, first, second, first_x, second_x, third, third_x, fourth, fourth_x), RELS


def whole_weights(full, plan):
    weights = []
    for (depth, width), first, part_width, parts in plan:
        block = full[:, :, first : first + part_width * parts]
        if parts > 1:
            owners, rows, _ = block.shape
            block = block.reshape(owners, rows, parts, part_width).transpose(0, 2, 1, 3)
        weights.append(block.reshape(depth, width))
    return weights, None


def add_split(left, right, picks):
    rest = left.shape[1:]

    def kernel(l_ref, r_ref, *outs):
        for out, pick in zip(outs, picks):
            for at, (a, b) in enumerate(pick):
                out[at] = (l_ref[a].astype(F32) + r_ref[b].astype(F32)).astype(out.dtype)

    return simple_call(kernel, [left, right], [sds((len(p),) + rest, BF16) for p in picks], "add_split")


def add_all(parts, dtype):
    def kernel(*refs):
        total = refs[0][...].astype(F32)
        for ref in refs[1:-1]:
            total += ref[...].astype(F32)
        refs[-1][...] = total.astype(dtype)

    (out,) = simple_call(kernel, parts, [sds(parts[0].shape, dtype)], "add_all")
    return out


def scatter_sum(keep, away, slc):
    owners = slc.owners
    (got,) = yield (slc.send(away, swap=1),)
    odd, even = add_split(
        keep,
        got,
        [[(j, j) for j in range(1, owners, 2)], [(j, j) for j in range(0, owners, 2)]],
    )
    got, even = yield (slc.send(odd, 1), even)
    blocks = add_split(even, got, [[(j, j)] for j in range(owners // 2)])
    arrived = yield (blocks[0],) + tuple(slc.send(blocks[j], 2 * j) for j in range(1, owners // 2))
    total = add_all(arrived, BF16)
    swap = 2
    while swap < slc.reps:
        total, got = yield (total, slc.send(total, swap=swap))
        total = add_all([total, got], BF16)
        swap *= 2
    total, other = yield (total, slc.send(total, swap=1))
    return total[0], other[0]


class Chain:
    def __init__(self, steps):
        self.steps, self.result = steps, None
        self.pending = next(steps)

    def step(self, arrived):
        try:
            self.pending = self.steps.send(arrived)
        except StopIteration as end:
            self.pending, self.result = None, end.value

    def finish(self):
        while self.pending is not None:
            self.step(self.pending)
        return self.result


def advance(chains, tied):
    live = [chain for chain in chains if chain.pending is not None]
    tied, arrived = lax.optimization_barrier((tied, [chain.pending for chain in live]))
    for chain, got in zip(live, arrived):
        chain.step(tuple(got))
    return tied


def unpack(halves, cols, owners, layers):
    rows, width, hidden = cols.rows, cols.width, cols.hidden

    def kernel(*refs):
        ins = refs[: 4 * layers]
        w_ada, b_ada, w_qkv, qv_bias, w_out, b_out, w_up, b_up, w_down, b_down, row_ref = refs[4 * layers :]
        me, core = my_place()

        def take(pair, first, size):
            half_width = pair[0].shape[-1]
            parts = []
            for half in range(2):
                lo, hi = max(first, half * half_width), min(first + size, (half + 1) * half_width)
                if lo < hi:
                    parts.append(pair[half][:, lo - half * half_width : hi - half * half_width])
            return jnp.concatenate(parts, axis=1).astype(F32) if len(parts) > 1 else parts[0].astype(F32)

        def write(layer, attn, mlp):
            w_ada[layer, :, : 3 * width] = take(attn, 0, 3 * width)
            w_qkv[layer] = take(attn, *cols.attn["qkv"])
            w_out[layer] = take(attn, *cols.attn["out"])
            w_ada[layer, :, 3 * width :] = take(mlp, 0, 3 * width)
            w_up[layer] = take(mlp, *cols.mlp["up"])
            for part in range(cols.parts):
                w_down[layer, part * rows : (part + 1) * rows, :] = take(
                    mlp, cols.mlp["down"][0] + part * width, width
                )
            at = 0
            for pair, first, size in (
                (attn, cols.attn_end, 6 * width),
                (mlp, cols.mlp_end, 4 * width + hidden),
            ):
                tiles = [
                    take(pair, first + t * LANES, LANES) for t in range(cols.tiles(size))
                ]
                for line in range(size // LANES):
                    row_ref[layer : layer + 1, at : at + LANES] = tiles[line // rows][
                        line % rows : line % rows + 1, :
                    ]
                    at += LANES

        for layer in range(layers):
            attn, mlp = ins[4 * layer : 4 * layer + 2], ins[4 * layer + 2 : 4 * layer + 4]

            @pl.when(core == 0)
            def _():
                write(layer, attn, mlp)

            @pl.when(core == 1)
            def _():
                write(layer, attn[::-1], mlp[::-1])

        w = width
        ada = jnp.concatenate([row_ref[:, : 3 * w], row_ref[:, 6 * w : 9 * w]], axis=1)
        qv = row_ref[:, 3 * w : 5 * w]
        out = row_ref[:, 5 * w : 6 * w]
        up = row_ref[:, 9 * w : 9 * w + hidden]
        down = row_ref[:, 9 * w + hidden : 10 * w + hidden]
        for owner in range(owners):

            @pl.when(me == owner)
            def _():
                for ref, value in ((b_ada, ada), (qv_bias, qv), (b_out, out), (b_up, up), (b_down, down)):
                    size = ref.shape[-1]
                    ref[...] = value[:, owner * size : (owner + 1) * size]

    outs = [
        sds((layers, rows, 6 * width)),
        sds((layers, 6 * width // owners)),
        sds((layers, rows, 3 * width)),
        sds((layers, 2 * width // owners)),
        sds((layers, rows, width)),
        sds((layers, width // owners)),
        sds((layers, rows, hidden)),
        sds((layers, hidden // owners)),
        sds((layers, rows * cols.parts, width)),
        sds((layers, width // owners)),
    ]
    args = [x for group in halves for x in group]
    return simple_call(
        kernel, args, outs, "unpack", [pltpu.VMEM((layers, 10 * width + hidden), F32)]
    )


def program(slc, latents, condition, cotangent, *stacked):
    layers = stacked[0].shape[0]
    width = latents.shape[-1]
    rows = stacked[2].shape[1]
    hidden = stacked[6].shape[-1]
    owners = slc.owners
    cols = Columns(rows, width, hidden)
    packed = pack_shards(stacked, cols, owners, layers)
    tiles = cols.tiles(layers * cols.bias_size) * LANES

    plans = []
    for layer in range(layers):
        base = 0 if layer == 0 else cols.attn_end
        plans.append((cols.attn_plan(), cols.mlp_plan(base)))
    s = jax.nn.silu(condition).astype(BF16)
    shared = can_share(slc, rows)
    if shared:
        now, chains = Chain(gather(packed[0], slc)), []
        waiting = list(packed[1:])
        waiting[0] = advance([now], waiting[0])
        chains.append(Chain(gather(waiting.pop(0), slc)))
        first = now.finish()
        bias_tiles = [piece[:, cols.attn_end :] for piece in first[0]]
        only_of = [only for _, _, only in first[1]]
    else:
        full = [lax.all_gather(piece, "fsdp", axis=0, tiled=False) for piece in packed]
        places = [(full[0], full[1])] + [(x, x) for x in full[2:]]
        whole_groups = [
            (whole_weights(a, pa), whole_weights(m, pm)) for (a, m), (pa, pm) in zip(places, plans)
        ]
        bias_tiles = [full[0][owner, :, cols.attn_end :] for owner in range(owners)]
        only_of = [None] * owners
    bias = sum_bias(bias_tiles, cols, layers, only_of)

    h = latents
    saved = []
    for layer in range(layers):
        attn_plan, mlp_plan = plans[layer]
        attn = (first if layer == 0 else chains[layer].finish()) if shared else whole_groups[layer][0]
        mod1, h2, qkv, p, o, y = attn_fwd(h, s, bias, attn, attn_plan, cols, layer)
        if shared and layer == 0:
            h2, waiting = advance(chains, (h2, waiting))
            chains += [Chain(gather(piece, slc)) for piece in waiting]
        if shared:
            mlp = chains[layer if layer else 0].finish()
        else:
            mlp = whole_groups[layer][1]
        mod2, h3, m, g, slope, z = mlp_fwd(h2, s, bias, mlp, mlp_plan, cols, layer)
        if shared:
            h3 = advance(chains, h3)
        saved.append((h, attn, mlp, mod1, h2, qkv, p, o, y, mod2, m, g, slope, z))
        h = h3
    output = h

    grad = cotangent
    grad_silu = None
    chains = []
    for layer in reversed(range(layers)):
        attn_plan, mlp_plan = plans[layer]
        h, attn, mlp, mod1, h2, qkv, p, o, y, mod2, m, g, slope, z = saved[layer]
        cond2, keep, away, grad = mlp_bwd(
            s, mod2, h2, grad, m, g, slope, z, mlp, mlp_plan, cols, owners
        )
        grad, keep, away = advance(chains, (grad, keep, away))
        chains.append(Chain(scatter_sum(keep, away, slc)))
        grad = advance(chains[-1:], grad)
        cond1, keep, away, grad = attn_bwd(
            s, mod1, h, grad, qkv, p, o, y, attn, attn_plan, cols, owners
        )
        grad, keep, away = advance(chains, (grad, keep, away))
        chains.append(Chain(scatter_sum(keep, away, slc)))
        grad = advance(chains[-1:], grad)
        both = cond1 + cond2
        grad_silu = both if grad_silu is None else grad_silu + both
    done = [chain.finish() for chain in chains]
    halves = [done[2 * (layers - 1 - layer) + 1] + done[2 * (layers - 1 - layer)] for layer in range(layers)]
    sigmoid_c = jax.nn.sigmoid(condition)
    grad_cond = grad_silu * sigmoid_c * (1.0 + condition * (1.0 - sigmoid_c))
    return (output, grad, grad_cond) + tuple(unpack(halves, cols, owners, layers))


def solution(mesh):
    rows3 = P(("fsdp", "rep"), None, None)
    rows2 = P(("fsdp", "rep"), None)
    pair = (P(None, "fsdp", None), P(None, "fsdp"))
    return jax.shard_map(
        functools.partial(program, Slice(mesh)),
        mesh=mesh,
        in_specs=(rows3, rows2, rows3) + pair * 5,
        out_specs=(rows3, rows3, rows2) + pair * 5,
        check_vma=False,
    )
```

```python
import functools

import jax
import jax.numpy as jnp
from jax import lax
from jax.experimental import pallas as pl
from jax.experimental.pallas import tpu as pltpu
from jax.sharding import PartitionSpec as P

GELU_C = 0.7978845608028654
GELU_A = 0.044715
EPS = 1e-06
HEAD = 64
LANES = 128
F32 = jnp.float32
BF16 = jnp.bfloat16


def dot(left, right, contract=((1,), (0,))):
    return lax.dot_general(left, right, (contract, ((), ())), preferred_element_type=F32)


def dot_t(left, right):
    return dot(left, right, ((1,), (1,)))


def row_mean(x):
    return jnp.sum(x, axis=-1, keepdims=True) * (1.0 / x.shape[-1])


def norm_rows(x):
    centered = x - row_mean(x)
    inverse = lax.rsqrt(row_mean(centered * centered) + EPS)
    return centered * inverse, inverse


def norm_back(grad, normed, inverse):
    return inverse * (grad - row_mean(grad) - normed * row_mean(grad * normed))


def col_sum(x):
    return jnp.sum(x, axis=0, keepdims=True)


def split_hi_lo(x):
    hi = x.astype(BF16)
    lo = (x - hi.astype(F32)).astype(BF16)
    return jnp.concatenate([hi, lo], axis=0)


def my_place():
    return lax.axis_index("fsdp"), lax.axis_index("rep") & 1


def weight_copies(pieces, rels, scratch, first, width, parts, sems):
    me, core = my_place()
    copies = []
    for piece, (rel_even, rel_odd, only) in zip(pieces, rels):
        rows = piece.shape[0]
        owner = me ^ jnp.where(core == 0, rel_even, rel_odd)
        for part in range(parts):
            start = pl.multiple_of((owner * parts + part) * rows, rows)
            copy = pltpu.make_async_copy(
                piece.at[:, pl.ds(first + part * width, width)],
                scratch.at[pl.ds(start, rows), :],
                sems.at[len(copies)],
            )
            copies.append((only, copy))
    return copies


def on_place(only, action):
    if only is None:
        action()
    else:
        _, core = my_place()
        pl.when(core == only)(action)


class Columns:
    def __init__(self, rows, width, hidden):
        self.rows, self.width, self.hidden = rows, width, hidden
        self.parts = hidden // width
        w = width
        self.attn = {"ada": (0, 3 * w), "qkv": (3 * w, 3 * w), "out": (6 * w, w)}
        self.mlp = {"ada": (0, 3 * w), "up": (3 * w, hidden), "down": (3 * w + hidden, hidden)}
        self.attn_end = 7 * w
        self.mlp_end = 3 * w + 2 * hidden
        sizes = (6 * w, 3 * w, w, hidden, w)
        names = ("ada", "qkv", "out", "up", "down")
        self.bias, at = {}, 0
        for name, size in zip(names, sizes):
            self.bias[name] = (at, size)
            at += size
        self.bias_size = at
        self.attn_sums = {"ada": (0, 3 * w), "qv": (3 * w, 2 * w), "out": (5 * w, w)}
        self.mlp_sums = {"ada": (0, 3 * w), "up": (3 * w, hidden), "down": (3 * w + hidden, w)}
        self.attn_grad = self.even(self.attn_end + self.tiles(6 * w) * LANES)
        self.mlp_grad = self.even(self.mlp_end + self.tiles(4 * w + hidden) * LANES)

    def tiles(self, size):
        return -(-size // (LANES * self.rows))

    def even(self, columns):
        return -(-columns // (2 * LANES)) * 2 * LANES

    def attn_plan(self, base=0):
        w = self.width
        return [
            ((w, 3 * w), base + self.attn["ada"][0], 3 * w, 1),
            ((w, 3 * w), base + self.attn["qkv"][0], 3 * w, 1),
            ((w, w), base + self.attn["out"][0], w, 1),
        ]

    def mlp_plan(self, base=0):
        w, hidden = self.width, self.hidden
        return [
            ((w, 3 * w), base + self.mlp["ada"][0], 3 * w, 1),
            ((w, hidden), base + self.mlp["up"][0], hidden, 1),
            ((hidden, w), base + self.mlp["down"][0], w, self.parts),
        ]


def put_grad(refs, owner, first, value):
    me, _ = my_place()
    half_width = refs[0].shape[-1]
    width = value.shape[-1]
    for half in range(2):
        lo, hi = max(first, half * half_width), min(first + width, (half + 1) * half_width)
        if lo < hi:
            refs[half][owner ^ me, :, lo - half * half_width : hi - half * half_width] = value[
                :, lo - first : hi - first
            ].astype(BF16)


def put_sums(refs, tile_ref, rows, first):
    owners = refs[0].shape[0]
    for block in range(tile_ref.shape[0] // rows):
        tile = tile_ref[block * rows : (block + 1) * rows, :]
        for owner in range(owners):
            put_grad(refs, owner, first + block * LANES, tile)


def fill_sums(tile_ref, sums):
    tile_ref[...] = jnp.zeros_like(tile_ref)
    at = 0
    for row in sums:
        for lo in range(0, row.shape[-1], LANES):
            tile_ref[at : at + 1, :] = row[:, lo : lo + LANES]
            at += 1


def by_core(keep_ref, away_ref, write):
    _, core = my_place()

    @pl.when(core == 0)
    def _():
        write((keep_ref, away_ref))

    @pl.when(core != 0)
    def _():
        write((away_ref, keep_ref))


AHEAD = 4
BACK = 1


def lane_masks(tokens):
    lane = lax.broadcasted_iota(jnp.int32, (tokens, LANES), 1)
    return lane < HEAD, lane >= HEAD


def weave(main, side):
    for _ in main:
        next(side, None)
    for _ in side:
        pass


def drain(stage):
    for _ in stage:
        pass


def attn_fwd_body(args, weights, outs, scratch, arrive):
    s_ref, b_ada, b_qkv, b_out, h_ref, next_ref = args
    w_ada, w_qkv, w_out = weights
    mod_ref, h2_ref, qkv_ref, p_ref, o_ref, y_ref = outs
    ready_ref = scratch[0]
    step = pl.program_id(0)
    last = pl.num_programs(0) - 1
    tokens, width = h_ref.shape[1:]
    masks = lane_masks(tokens)
    zero = jnp.zeros((), BF16)

    def project(source, row, slot):
        mod = mod_ref[pl.ds(row, 1), :]
        shift, scale = mod[:, :width], mod[:, width : 2 * width]
        normed, _ = norm_rows(source[0])
        a = (normed * (1.0 + scale) + shift).astype(BF16)
        yield
        for first in range(0, 3 * width, 512):
            span = slice(first, min(first + 512, 3 * width))
            ready_ref[slot, :, span] = (dot(a, w_qkv[:, span]) + b_qkv[:, span]).astype(BF16)
            yield

    def attend(row, slot):
        def scores_of(head):
            lo = head // 2 * LANES
            query = ready_ref[slot, :, lo : lo + LANES] * jnp.asarray(0.125, BF16)
            key = ready_ref[slot, :, width + lo : width + lo + LANES]
            return dot_t(query, jnp.where(masks[head % 2], key, zero))

        def mix(head, p):
            lo = 2 * width + head // 2 * LANES
            value = ready_ref[slot, :, lo : lo + LANES]
            return dot(p, jnp.where(masks[head % 2], value, zero))

        heads = width // HEAD
        ahead = [scores_of(head) for head in range(AHEAD)]
        qkv_ref[0] = ready_ref[slot]
        parts, p_b = [], None
        for head in range(heads):
            scores = ahead.pop(0)
            if head + AHEAD < heads:
                ahead.append(scores_of(head + AHEAD))
            top = jnp.max(scores, axis=-1, keepdims=True)
            grown = jnp.exp(scores - top)
            if head:
                parts.append(mix(head - 1, p_b))
            p = grown * (1.0 / jnp.sum(grown, axis=-1, keepdims=True))
            p_ref[0, head] = p
            p_b = p.astype(BF16)
            yield
        parts.append(mix(heads - 1, p_b))
        attended = [(parts[i] + parts[i + 1]).astype(BF16) for i in range(0, heads, 2)]
        o = jnp.concatenate(attended, axis=1)
        o_ref[0] = o
        y = dot(o, w_out[...]) + b_out
        y_ref[0] = y
        gate = mod_ref[pl.ds(row, 1), 2 * width : 3 * width]
        h2_ref[0] = h_ref[0] + gate * y

    @pl.when(step == 0)
    def _():
        arrive(0)
        mod_ref[...] = dot(s_ref[...], w_ada[...]) + b_ada
        arrive(1)
        drain(project(h_ref, 0, 0))
        arrive(2)

    weave(
        attend(step, step & 1), project(next_ref, jnp.minimum(step + 1, last), (step + 1) & 1)
    )


def gelu_half(u):
    square = u * u
    t = jnp.tanh(u * (GELU_C + (GELU_C * GELU_A) * square))
    return 0.5 * t + 0.5, square


def mlp_fwd_body(args, weights, outs, scratch, arrive, chunk):
    s_ref, b_ada, b_up, b_down, h2_ref, next_ref = args
    w_ada, w_up, w_down = weights
    mod_ref, h3_ref, m_ref, u_ref, z_ref = outs
    ready_ref = scratch[0]
    step = pl.program_id(0)
    last = pl.num_programs(0) - 1
    width = h2_ref.shape[-1]
    hidden = w_up.shape[-1]
    spans = [slice(first, first + chunk) for first in range(0, hidden, chunk)]

    def prepare(source, row, slot):
        mod = mod_ref[pl.ds(row, 1), :]
        shift, scale = mod[:, :width], mod[:, width : 2 * width]
        normed, _ = norm_rows(source[0])
        ready_ref[slot] = (normed * (1.0 + scale) + shift).astype(BF16)
        yield

    def feed(row, slot):
        m = ready_ref[slot]
        m_ref[0] = m
        z = None
        u = dot(m, w_up[:, spans[0]]) + b_up[:, spans[0]]
        for at, span in enumerate(spans):
            later = None
            if at + 1 < len(spans):
                later = dot(m, w_up[:, spans[at + 1]]) + b_up[:, spans[at + 1]]
            half, _ = gelu_half(u)
            u_ref[0, :, span] = u
            part = dot((u * half).astype(BF16), w_down[span, :])
            z = part if z is None else z + part
            u = later
            yield
        z = z + b_down
        z_ref[0] = z
        gate = mod_ref[pl.ds(row, 1), 2 * width : 3 * width]
        h3_ref[0] = h2_ref[0] + gate * z

    @pl.when(step == 0)
    def _():
        arrive(0)
        mod_ref[...] = dot(s_ref[...], w_ada[...]) + b_ada
        drain(prepare(h2_ref, 0, 0))
        arrive(1)
        arrive(2)

    weave(feed(step, step & 1), prepare(next_ref, jnp.minimum(step + 1, last), (step + 1) & 1))


def mlp_bwd_body(args, weights, outs, accs, arrive, chunk, cols):
    s_ref, mod_ref, dh3_ref, m_ref, u_ref, h2_ref, dh3_before, z_ref = args
    w_ada, w_up, w_down = weights
    dcond_ref, keep_ref, away_ref, dh2_ref = outs
    acc_up, acc_down, dmod_ref, bias_ref, tile_ref, ada_ref, down_ref, dm_ref = accs
    step = pl.program_id(0)
    last = pl.num_programs(0) - 1
    width = h2_ref.shape[-1]
    hidden = w_up.shape[-1]
    spans = [slice(first, first + chunk) for first in range(0, hidden, chunk)]

    def products(row, slot):
        gate = mod_ref[pl.ds(row, 1), 2 * width : 3 * width]
        dz = gate * dh3_ref[0]
        dzb = dz.astype(BF16)
        dg = dot_t(dzb, w_down[spans[0], :])
        dzb_t = dzb.T
        m_t = m_ref[0].T
        bias_ref[:, hidden : hidden + width] += col_sum(dz)
        dm = None
        for at, span in enumerate(spans):
            later = dot_t(dzb, w_down[spans[at + 1], :]) if at + 1 < len(spans) else None
            u = u_ref[0, :, span]
            half, square = gelu_half(u)
            g = u * half
            slope = half + (g - g * half) * (2.0 * GELU_C + (6.0 * GELU_C * GELU_A) * square)
            du = dg * slope
            dub = du.astype(BF16)
            acc_down[:, span] += dot(dzb_t, g.astype(BF16))
            bias_ref[:, span] += col_sum(du)
            acc_up[:, span] += dot(m_t, dub)
            part = dot_t(dub, w_up[:, span])
            dm = part if dm is None else dm + part
            dg = later
            yield
        dm_ref[slot] = dm

    def finish(row, slot):
        dm = dm_ref[slot]
        dh3 = dh3_before[0]
        scale = mod_ref[pl.ds(row, 1), width : 2 * width]
        normed, inverse = norm_rows(h2_ref[0])
        yield
        dmod_ref[pl.ds(row, 1), :] = jnp.concatenate(
            [col_sum(dm), col_sum(dm * normed), col_sum(dh3 * z_ref[0])], axis=1
        )
        dh2_ref[0] = dh3 + norm_back(dm * (1.0 + scale), normed, inverse)
        yield

    @pl.when(step == 0)
    def _():
        acc_up[...] = jnp.zeros_like(acc_up)
        acc_down[...] = jnp.zeros_like(acc_down)
        bias_ref[...] = jnp.zeros_like(bias_ref)
        dm_ref[...] = jnp.zeros_like(dm_ref)
        arrive(2)
        arrive(1)

    before = jnp.maximum(step - 1, 0)

    @pl.when(step < last)
    def _():
        weave(products(step, step & 1), finish(before, (step + 1) & 1))

    @pl.when(step == last)
    def _():
        drain(finish(before, (step + 1) & 1))
        arrive(0)
        ada = ada_tail(s_ref, w_ada, dmod_ref, dcond_ref)
        ada_ref[...] = ada
        down_ref[...] = acc_down[...].T
        fill_sums(tile_ref, [col_sum(dmod_ref[...]), bias_ref[...]])
        rows = cols.rows

        def write(refs):
            for owner in range(refs[0].shape[0]):
                mine = slice(owner * rows, (owner + 1) * rows)
                put_grad(refs, owner, 0, ada_ref[mine, :])
                put_grad(refs, owner, cols.mlp["up"][0], acc_up[mine, :])
                for part in range(cols.parts):
                    first = (owner * cols.parts + part) * rows
                    put_grad(
                        refs,
                        owner,
                        cols.mlp["down"][0] + part * width,
                        down_ref[first : first + rows, :],
                    )
            put_sums(refs, tile_ref, rows, cols.mlp_end)

        by_core(keep_ref, away_ref, write)


def ada_tail(s_ref, w_ada, dmod_ref, dcond_ref):
    parts = split_hi_lo(dmod_ref[...])
    rows = dmod_ref.shape[0]
    both = dot_t(parts, w_ada[...])
    dcond_ref[...] = both[:rows] + both[rows:]
    s = s_ref[...]
    return dot(jnp.concatenate([s, s], axis=0), parts, ((0,), (0,)))


def attn_bwd_body(args, weights, outs, accs, arrive, cols):
    s_ref, mod_ref, dh2_ref, qkv_ref, p_ref, o_ref, h_ref, dh2_before, y_ref = args
    w_ada, w_qkv, w_out = weights
    dcond_ref, keep_ref, away_ref, dh_ref = outs
    acc_qkv, acc_out, dqkv_ref, dmod_ref, bias_ref, tile_ref, ada_ref = accs
    step = pl.program_id(0)
    last = pl.num_programs(0) - 1
    tokens, width = h_ref.shape[1:]
    masks = lane_masks(tokens)
    zero = jnp.zeros((), BF16)
    heads = width // HEAD

    def attend(row, slot):
        gate = mod_ref[pl.ds(row, 1), 2 * width : 3 * width]
        dy = gate * dh2_ref[0]
        dyb = dy.astype(BF16)
        do = dot_t(dyb, w_out[...]).astype(BF16)
        bias_ref[:, 2 * width : 3 * width] += col_sum(dy)
        query_t = qkv_ref[0, :, :width].T * jnp.asarray(0.125, BF16)
        yield

        def grad_of(head):
            lo = head // 2 * LANES
            value = qkv_ref[0, :, 2 * width + lo : 2 * width + lo + LANES]
            return dot_t(do[:, lo : lo + LANES], jnp.where(masks[head % 2], value, zero))

        ahead = [grad_of(head) for head in range(BACK)]
        do_t = do.T
        acc_out[...] += dot(o_ref[0].T, dyb)
        dk_t, dv_t, dqs, ds = [], [], [], None

        def through(head, ds):
            rows = slice(head * HEAD, (head + 1) * HEAD)
            lo = width + head // 2 * LANES
            key = qkv_ref[0, :, lo : lo + LANES] * jnp.asarray(0.125, BF16)
            dk_t.append(dot(query_t[rows], ds))
            dqs.append(dot(ds, jnp.where(masks[head % 2], key, zero)))
            if head % 2:
                lo -= width
                dq = dqs[-2] + dqs[-1]
                bias_ref[:, lo : lo + LANES] += col_sum(dq)
                dqkv_ref[slot, :, lo : lo + LANES] = dq.astype(BF16)

        for head in range(heads):
            dp = ahead.pop(0)
            if head + BACK < heads:
                ahead.append(grad_of(head + BACK))
            p = p_ref[0, head]
            dv_t.append(dot(do_t[head * HEAD : (head + 1) * HEAD], p.astype(BF16)))
            inner = jnp.sum(p * dp, axis=-1, keepdims=True)
            if head:
                through(head - 1, ds)
            ds = (p * (dp - inner)).astype(BF16)
            yield
        through(heads - 1, ds)
        dv = jnp.concatenate(dv_t, axis=0).T
        bias_ref[:, width : 2 * width] += col_sum(dv)
        dqkv_ref[slot, :, width : 2 * width] = jnp.concatenate(dk_t, axis=0).T.astype(BF16)
        dqkv_ref[slot, :, 2 * width :] = dv.astype(BF16)

    def finish(row, slot):
        mod = mod_ref[pl.ds(row, 1), :]
        shift, scale = mod[:, :width], mod[:, width : 2 * width]
        da = dot_t(dqkv_ref[slot], w_qkv[...])
        normed, inverse = norm_rows(h_ref[0])
        a_t = (normed * (1.0 + scale) + shift).astype(BF16).T
        yield
        dh2 = dh2_before[0]
        for first in range(0, 3 * width, 256):
            span = slice(first, min(first + 256, 3 * width))
            acc_qkv[:, span] += dot(a_t, dqkv_ref[slot, :, span])
            yield
        dmod_ref[pl.ds(row, 1), :] = jnp.concatenate(
            [col_sum(da), col_sum(da * normed), col_sum(dh2 * y_ref[0])], axis=1
        )
        dh_ref[0] = dh2 + norm_back(da * (1.0 + scale), normed, inverse)
        yield

    @pl.when(step == 0)
    def _():
        acc_qkv[...] = jnp.zeros_like(acc_qkv)
        acc_out[...] = jnp.zeros_like(acc_out)
        bias_ref[...] = jnp.zeros_like(bias_ref)
        dqkv_ref[...] = jnp.zeros_like(dqkv_ref)
        arrive(2)
        arrive(1)

    before = jnp.maximum(step - 1, 0)

    @pl.when(step < last)
    def _():
        weave(attend(step, step & 1), finish(before, (step + 1) & 1))

    @pl.when(step == last)
    def _():
        drain(finish(before, (step + 1) & 1))
        arrive(0)
        ada = ada_tail(s_ref, w_ada, dmod_ref, dcond_ref)
        ada_ref[...] = ada
        fill_sums(tile_ref, [col_sum(dmod_ref[...]), bias_ref[...]])
        rows = cols.rows

        def write(refs):
            for owner in range(refs[0].shape[0]):
                mine = slice(owner * rows, (owner + 1) * rows)
                put_grad(refs, owner, 0, ada_ref[mine, :])
                put_grad(refs, owner, cols.attn["qkv"][0], acc_qkv[mine, :])
                put_grad(refs, owner, cols.attn["out"][0], acc_out[mine, :])
            put_sums(refs, tile_ref, rows, cols.attn_end)

        by_core(keep_ref, away_ref, write)


def per_latent(shape, ahead=0):
    rest = shape[1:]

    def place(b):
        return (jnp.clip(b + ahead, 0, shape[0] - 1),) + (0,) * len(rest)

    return pl.BlockSpec((1,) + rest, place)


def whole(shape):
    return pl.BlockSpec(shape, lambda b: (0,) * len(shape))


def sds(shape, dtype=F32):
    return jax.ShapeDtypeStruct(tuple(shape), dtype)


def params():
    return pltpu.CompilerParams(dimension_semantics=("arbitrary",), vmem_limit_bytes=60 * 2**20)


def estimate(micros):
    return pl.CostEstimate(flops=int(micros * 1.0e9), bytes_accessed=int(micros * 1.0e6), transcendentals=0)


def run(body, constants, streams, gathered, plan, out_constants, out_streams, scratch, name, micros, order, more=0, behind=0):
    streams, shifts = zip(*streams)
    latents = streams[0].shape[0]
    pieces, rels = gathered
    direct = rels is None
    n_in = len(constants) + len(streams)
    n_out = len(out_streams) + len(out_constants)
    def kernel(*refs):
        ins, rest = refs[:n_in], refs[n_in:]
        got, rest = rest[: len(pieces)], rest[len(pieces) :]
        outs, rest = rest[:n_out], rest[n_out:]
        if direct:
            weights, accs = got, rest
        else:
            count = len(plan)
            weights, sems, accs = rest[:count], rest[count : 2 * count], rest[2 * count :]

        def copies_of(at):
            _, first, width, parts = plan[at]
            return weight_copies(got, rels, weights[at], first, width, parts, sems[at])

        def arrive(at):
            if not direct:
                for only, copy in copies_of(at):
                    on_place(only, copy.wait)

        if not direct:

            @pl.when(pl.program_id(0) == 0)
            def _():
                for at in order:
                    for only, copy in copies_of(at):
                        on_place(only, copy.start)

        body(ins, weights, outs, accs, got, arrive)

    if direct:
        piece_specs = [whole(p.shape) for p in pieces]
        extra = []
    else:
        piece_specs = [pl.BlockSpec(memory_space=pltpu.HBM)] * len(pieces)
        extra = [pltpu.VMEM(shape, BF16) for shape, _, _, _ in plan]
        extra += [pltpu.SemaphoreType.DMA((len(pieces) * parts,)) for _, _, _, parts in plan]
    return pl.pallas_call(
        kernel,
        grid=(latents + more,),
        in_specs=[whole(c.shape) for c in constants]
        + [per_latent(x.shape, ahead) for x, ahead in zip(streams, shifts)]
        + piece_specs,
        out_specs=[whole(x.shape) for x in out_constants]
        + [per_latent(x.shape, behind) for x in out_streams],
        out_shape=list(out_constants) + list(out_streams),
        scratch_shapes=extra + list(scratch),
        compiler_params=params(),
        cost_estimate=estimate(micros),
        name=name,
    )(*constants, *streams, *pieces)


def layer_bias(bias_ref, cols, layer, name, part=None):
    first, size = cols.bias[name]
    first += layer * cols.bias_size
    if part is not None:
        size //= 2
        first += part * size
    return bias_ref[:, first : first + size]


def attn_fwd(h, s, bias, gathered, plan, cols, layer, layers=1):
    n, tokens, width = h.shape
    here = bias is None
    lines = layers * cols.bias_size // LANES
    tiles = cols.tiles(layers * cols.bias_size)
    pieces = gathered[0]

    def body(ins, weights, outs, accs, got, arrive):
        if here:
            (s_ref, h_ref, next_ref), bias_ref, outs = ins, outs[0], outs[1:]
            tile_ref, sems = accs[1:]

            @pl.when(pl.program_id(0) == 0)
            def _():
                copies = [
                    pltpu.make_async_copy(
                        piece.at[:, pl.ds(cols.attn_end, tiles * LANES)],
                        tile_ref.at[at],
                        sems.at[at],
                    )
                    for at, piece in enumerate(got)
                ]
                for copy in copies:
                    copy.start()
                for copy in copies:
                    copy.wait()
                for at, line in enumerate(bias_row(tile_ref[...], cols.rows, lines)):
                    bias_ref[:, at * LANES : (at + 1) * LANES] = line

        else:
            s_ref, bias_ref, h_ref, next_ref = ins
        biases = (
            layer_bias(bias_ref, cols, layer, "ada", 0),
            layer_bias(bias_ref, cols, layer, "qkv"),
            layer_bias(bias_ref, cols, layer, "out"),
        )
        attn_fwd_body((s_ref,) + biases + (h_ref, next_ref), weights, outs, accs, arrive)

    scratch = [
        pltpu.VMEM((2, tokens, 3 * width), BF16),
        pltpu.VMEM((len(pieces), cols.rows, tiles * LANES), BF16),
        pltpu.SemaphoreType.DMA((len(pieces),)),
    ]
    outs = run(
        body,
        [s] if here else [s, bias],
        [(h, 0), (h, 1)],
        gathered,
        plan,
        ([sds((1, lines * LANES))] if here else []) + [sds((n, 3 * width))],
        [
            sds(h.shape),
            sds((n, tokens, 3 * width), BF16),
            sds((n, width // HEAD, tokens, tokens)),
            sds(h.shape, BF16),
            sds(h.shape),
        ],
        scratch if here else scratch[:1],
        "attn_fwd",
        20,
        (0, 1, 2),
    )
    return outs if here else [bias] + list(outs)


def mlp_fwd(h2, s, bias, gathered, plan, cols, layer, chunk=512):
    n, tokens, width = h2.shape
    hidden = cols.hidden

    def body(ins, weights, outs, accs, got, arrive):
        s_ref, bias_ref, h2_ref, next_ref = ins
        biases = (
            layer_bias(bias_ref, cols, layer, "ada", 1),
            layer_bias(bias_ref, cols, layer, "up"),
            layer_bias(bias_ref, cols, layer, "down"),
        )
        mlp_fwd_body((s_ref,) + biases + (h2_ref, next_ref), weights, outs, accs, arrive, chunk)

    return run(
        body,
        [s, bias],
        [(h2, 0), (h2, 1)],
        gathered,
        plan,
        [sds((n, 3 * width))],
        [sds(h2.shape), sds(h2.shape, BF16), sds((n, tokens, hidden)), sds(h2.shape)],
        [pltpu.VMEM((2, tokens, width), BF16)],
        "mlp_fwd",
        22,
        (0, 1, 2),
    )


def mlp_bwd(s, mod, h2, dh3, m, u, z, gathered, plan, cols, owners, chunk=256):
    n, tokens, width = h2.shape
    hidden = cols.hidden

    def body(ins, weights, outs, accs, got, arrive):
        mlp_bwd_body(ins, weights, outs, accs, arrive, chunk, cols)

    return run(
        body,
        [s, mod],
        [(dh3, 0), (m, 0), (u, 0), (h2, -1), (dh3, -1), (z, -1)],
        gathered,
        plan,
        [sds((n, width))] + [sds((owners, cols.rows, cols.mlp_grad // 2), BF16)] * 2,
        [sds(h2.shape)],
        [
            pltpu.VMEM((width, hidden), F32),
            pltpu.VMEM((width, hidden), F32),
            pltpu.VMEM((n, 3 * width), F32),
            pltpu.VMEM((1, hidden + width), F32),
            pltpu.VMEM((cols.tiles(4 * width + hidden) * cols.rows, LANES), F32),
            pltpu.VMEM((width, 3 * width), F32),
            pltpu.VMEM((hidden, width), F32),
            pltpu.VMEM((2, tokens, width), F32),
        ],
        "mlp_bwd",
        24,
        (2, 1, 0),
        more=1,
        behind=-1,
    )


def attn_bwd(s, mod, h, dh2, qkv, p, o, y, gathered, plan, cols, owners):
    n, tokens, width = h.shape

    def body(ins, weights, outs, accs, got, arrive):
        attn_bwd_body(ins, weights, outs, accs, arrive, cols)

    return run(
        body,
        [s, mod],
        [(dh2, 0), (qkv, 0), (p, 0), (o, 0), (h, -1), (dh2, -1), (y, -1)],
        gathered,
        plan,
        [sds((n, width))] + [sds((owners, cols.rows, cols.attn_grad // 2), BF16)] * 2,
        [sds(h.shape)],
        [
            pltpu.VMEM((width, 3 * width), F32),
            pltpu.VMEM((width, width), F32),
            pltpu.VMEM((2, tokens, 3 * width), BF16),
            pltpu.VMEM((n, 3 * width), F32),
            pltpu.VMEM((1, 3 * width), F32),
            pltpu.VMEM((cols.tiles(6 * width) * cols.rows, LANES), F32),
            pltpu.VMEM((width, 3 * width), F32),
        ],
        "attn_bwd",
        28,
        (2, 1, 0),
        more=1,
        behind=-1,
    )


def simple_call(kernel, args, outs, name, scratch=()):
    return pl.pallas_call(
        kernel,
        grid=(1,),
        in_specs=[whole(x.shape) for x in args],
        out_specs=[whole(x.shape) for x in outs],
        out_shape=list(outs),
        scratch_shapes=list(scratch),
        compiler_params=params(),
        cost_estimate=estimate(1),
        name=name,
    )(*args)


def pack_shards(stacked, cols, owners, layers):
    rows, width, hidden = cols.rows, cols.width, cols.hidden
    tiles = cols.tiles(layers * cols.bias_size)
    names = ("ada", "qkv", "out", "up", "down")

    def kernel(w_ada, b_ada, w_qkv, qv_bias, w_out, b_out, w_up, b_up, w_down, b_down, *refs):
        outs, row_ref, tile_ref = refs[:-2], refs[-2], refs[-1]
        me, _ = my_place()
        for layer in range(layers):
            attn_ref, mlp_ref = outs[2 * layer], outs[2 * layer + 1]
            attn_ref[:, : 3 * width] = w_ada[layer, :, : 3 * width]
            attn_ref[:, 3 * width : 6 * width] = w_qkv[layer]
            attn_ref[:, 6 * width : 7 * width] = w_out[layer]
            mlp_ref[:, : 3 * width] = w_ada[layer, :, 3 * width :]
            first = 3 * width
            mlp_ref[:, first : first + hidden] = w_up[layer]
            first += hidden
            for part in range(cols.parts):
                mlp_ref[:, first + part * width : first + (part + 1) * width] = w_down[
                    layer, part * rows : (part + 1) * rows, :
                ]
        row_ref[...] = jnp.zeros_like(row_ref)
        for owner in range(owners):

            @pl.when(me == owner)
            def _():
                for layer in range(layers):
                    for name, ref in zip(names, (b_ada, qv_bias, b_out, b_up, b_down)):
                        size = ref.shape[-1]
                        at = layer * cols.bias_size + cols.bias[name][0] + owner * size
                        if name == "qkv" and 2 * owner >= owners:
                            at += width
                        row_ref[:, at : at + size] = ref[layer : layer + 1, :].astype(F32)

        tile_ref[...] = jnp.zeros_like(tile_ref)
        for at in range(layers * cols.bias_size // LANES):
            tile_ref[at : at + 1, :] = row_ref[:, at * LANES : (at + 1) * LANES]
        for tile in range(tiles):
            outs[0][:, cols.attn_end + tile * LANES : cols.attn_end + (tile + 1) * LANES] = tile_ref[
                tile * rows : (tile + 1) * rows, :
            ].astype(BF16)

    outs = [sds((rows, cols.attn_end + tiles * LANES), BF16), sds((rows, cols.mlp_end), BF16)]
    outs += [sds((rows, cols.attn_end), BF16), sds((rows, cols.mlp_end), BF16)] * (layers - 1)
    scratch = [pltpu.VMEM((1, layers * cols.bias_size), F32), pltpu.VMEM((tiles * rows, LANES), F32)]
    return simple_call(kernel, stacked, outs, "pack", scratch)


def bias_row(tiles, rows, lines):
    total = jnp.sum(tiles.astype(F32), axis=0)
    return [
        total[at % rows : at % rows + 1, at // rows * LANES : (at // rows + 1) * LANES]
        for at in range(lines)
    ]


class Slice:
    def __init__(self, mesh):
        self.owners, self.reps = mesh.shape["fsdp"], mesh.shape["rep"]

    def send(self, x, rel_even=0, rel_odd=None, swap=0, only=None):
        rel_odd = rel_even if rel_odd is None else rel_odd
        pairs = []
        for f in range(self.owners):
            for r in range(self.reps):
                rel = rel_odd if r & 1 else rel_even
                if only is None or (r & 1) == only:
                    pairs.append((f * self.reps + r, (f ^ rel) * self.reps + (r ^ swap)))
        return lax.ppermute(x, ("fsdp", "rep"), pairs)


def can_share(slc, rows):
    return slc.owners == 8 and slc.reps % 2 == 0 and rows % 16 == 0


RELS = (
    (0, 0, None),
    (2, 4, None),
    (6, 1, None),
    (4, 2, None),
    (1, 6, None),
    (3, 5, None),
    (5, 3, None),
    (7, 7, 0),
    (7, 7, 1),
)


def gather(piece, slc):
    first, second = yield (slc.send(piece, 2, 4), slc.send(piece, 6, 1))
    first_x, second_x = slc.send(first, swap=1), slc.send(second, swap=1)
    third, fourth = slc.send(first, 1, 1), slc.send(second, 1, only=0)
    first_x, second_x, third, fourth = yield (first_x, second_x, third, fourth)
    third_x, fourth_x = yield (slc.send(third, swap=1), slc.send(fourth, swap=1, only=0))
    return (piece, first, second, first_x, second_x, third, third_x, fourth, fourth_x)


def whole_weights(full, plan):
    weights = []
    for (depth, width), first, part_width, parts in plan:
        block = full[:, :, first : first + part_width * parts]
        if parts > 1:
            owners, rows, _ = block.shape
            block = block.reshape(owners, rows, parts, part_width).transpose(0, 2, 1, 3)
        weights.append(block.reshape(depth, width))
    return weights, None


def add_up(parts):
    total = parts[0].astype(F32)
    for part in parts[1:]:
        total = total + part.astype(F32)
    return total.astype(BF16)


def scatter_sum(keep, away, slc):
    owners = slc.owners
    keep, near = yield (keep, slc.send(away, swap=1))
    odd = add_up([keep[1::2], near[1::2]])
    keep, near, across = yield (keep, near, slc.send(odd, 1))
    mine = [(keep[2 * j], near[2 * j], across[j]) for j in range(owners // 2)]
    far = [slc.send(add_up(mine[j]), 2 * j) for j in range(1, owners // 2)]
    keep, near, across, *far = yield (keep, near, across, *far)
    total = add_up([keep[0], near[0], across[0], *far])
    swap = 2
    while swap < slc.reps:
        total, got = yield (total, slc.send(total, swap=swap))
        total = add_up([total, got])
        swap *= 2
    total, other = yield (total, slc.send(total, swap=1))
    return total, other


class Chain:
    def __init__(self, steps):
        self.steps, self.result = steps, None
        self.pending = next(steps)

    def step(self, arrived):
        try:
            self.pending = self.steps.send(arrived)
        except StopIteration as end:
            self.pending, self.result = None, end.value

    def finish(self):
        while self.pending is not None:
            self.step(self.pending)
        return self.result


def advance(chains, tied):
    live = [chain for chain in chains if chain.pending is not None]
    tied, arrived = lax.optimization_barrier((tied, [chain.pending for chain in live]))
    for chain, got in zip(live, arrived):
        chain.step(tuple(got))
    return tied


def unpack(halves, cols, owners, layers):
    rows, width, hidden = cols.rows, cols.width, cols.hidden

    def kernel(*refs):
        ins = refs[: 4 * layers]
        w_ada, b_ada, w_qkv, qv_bias, w_out, b_out, w_up, b_up, w_down, b_down, row_ref = refs[4 * layers :]
        me, core = my_place()

        def take(pair, first, size):
            half_width = pair[0].shape[-1]
            parts = []
            for half in range(2):
                lo, hi = max(first, half * half_width), min(first + size, (half + 1) * half_width)
                if lo < hi:
                    parts.append(pair[half][:, lo - half * half_width : hi - half * half_width])
            return jnp.concatenate(parts, axis=1).astype(F32) if len(parts) > 1 else parts[0].astype(F32)

        def write(layer, attn, mlp):
            w_ada[layer, :, : 3 * width] = take(attn, 0, 3 * width)
            w_qkv[layer] = take(attn, *cols.attn["qkv"])
            w_out[layer] = take(attn, *cols.attn["out"])
            w_ada[layer, :, 3 * width :] = take(mlp, 0, 3 * width)
            w_up[layer] = take(mlp, *cols.mlp["up"])
            for part in range(cols.parts):
                w_down[layer, part * rows : (part + 1) * rows, :] = take(
                    mlp, cols.mlp["down"][0] + part * width, width
                )
            at = 0
            for pair, first, size in (
                (attn, cols.attn_end, 6 * width),
                (mlp, cols.mlp_end, 4 * width + hidden),
            ):
                tiles = [
                    take(pair, first + t * LANES, LANES) for t in range(cols.tiles(size))
                ]
                for line in range(size // LANES):
                    row_ref[layer : layer + 1, at : at + LANES] = tiles[line // rows][
                        line % rows : line % rows + 1, :
                    ]
                    at += LANES

        for layer in range(layers):
            attn, mlp = ins[4 * layer : 4 * layer + 2], ins[4 * layer + 2 : 4 * layer + 4]

            @pl.when(core == 0)
            def _():
                write(layer, attn, mlp)

            @pl.when(core == 1)
            def _():
                write(layer, attn[::-1], mlp[::-1])

        w = width
        ada = jnp.concatenate([row_ref[:, : 3 * w], row_ref[:, 6 * w : 9 * w]], axis=1)
        qv = row_ref[:, 3 * w : 5 * w]
        out = row_ref[:, 5 * w : 6 * w]
        up = row_ref[:, 9 * w : 9 * w + hidden]
        down = row_ref[:, 9 * w + hidden : 10 * w + hidden]
        for owner in range(owners):

            @pl.when(me == owner)
            def _():
                for ref, value in ((b_ada, ada), (qv_bias, qv), (b_out, out), (b_up, up), (b_down, down)):
                    size = ref.shape[-1]
                    ref[...] = value[:, owner * size : (owner + 1) * size]

    outs = [
        sds((layers, rows, 6 * width)),
        sds((layers, 6 * width // owners)),
        sds((layers, rows, 3 * width)),
        sds((layers, 2 * width // owners)),
        sds((layers, rows, width)),
        sds((layers, width // owners)),
        sds((layers, rows, hidden)),
        sds((layers, hidden // owners)),
        sds((layers, rows * cols.parts, width)),
        sds((layers, width // owners)),
    ]
    args = [x for group in halves for x in group]
    return simple_call(
        kernel, args, outs, "unpack", [pltpu.VMEM((layers, 10 * width + hidden), F32)]
    )


def program(slc, latents, condition, cotangent, *stacked):
    layers = stacked[0].shape[0]
    width = latents.shape[-1]
    rows = stacked[2].shape[1]
    hidden = stacked[6].shape[-1]
    owners = slc.owners
    cols = Columns(rows, width, hidden)
    packed = pack_shards(stacked, cols, owners, layers)
    attn_plan, mlp_plan = cols.attn_plan(), cols.mlp_plan()
    plans = [attn_plan, mlp_plan] * layers
    s = jax.nn.silu(condition).astype(BF16)
    h = latents
    shared = can_share(slc, rows)
    chains, waiting, bias = [], list(packed), None

    def begin():
        if waiting:
            chains.append(Chain(gather(waiting.pop(0), slc)))

    if shared:
        begin()
        waiting = advance(chains, waiting)
        begin()
        first = chains[0].finish()
        h, s, waiting, first = advance(chains[1:], (h, s, waiting, first))
        begin()
        begin()
    else:
        full = [lax.all_gather(piece, "fsdp", axis=0, tiled=False) for piece in packed]
        ready = [whole_weights(x, plan) for x, plan in zip(full, plans)]
        lines = layers * cols.bias_size // LANES
        bias = jnp.concatenate(bias_row(full[0][:, :, cols.attn_end :], rows, lines), axis=1)

    def weights_of(group, tied):
        if not shared:
            return ready[group], tied
        if group == 0:
            return (first, RELS), tied
        tied, moving = advance(chains[group : group + 2], (tied, waiting))
        waiting[:] = moving
        begin()
        return (chains[group].finish(), RELS), tied

    saved = []
    for layer in range(layers):
        attn, h = weights_of(2 * layer, h)
        bias, mod1, h2, qkv, p, o, y = attn_fwd(h, s, bias, attn, attn_plan, cols, layer, layers)
        mlp, h2 = weights_of(2 * layer + 1, h2)
        mod2, h3, m, u, z = mlp_fwd(h2, s, bias, mlp, mlp_plan, cols, layer)
        saved.append((h, attn, mlp, mod1, h2, qkv, p, o, y, mod2, m, u, z))
        h = h3
    output = h

    grad = cotangent
    grad_silu = None
    chains = []
    for layer in reversed(range(layers)):
        h, attn, mlp, mod1, h2, qkv, p, o, y, mod2, m, u, z = saved[layer]
        cond2, keep, away, grad = mlp_bwd(
            s, mod2, h2, grad, m, u, z, mlp, mlp_plan, cols, owners
        )
        grad, keep, away = advance(chains, (grad, keep, away))
        chains.append(Chain(scatter_sum(keep, away, slc)))
        grad = advance(chains[-1:], grad)
        cond1, keep, away, grad = attn_bwd(
            s, mod1, h, grad, qkv, p, o, y, attn, attn_plan, cols, owners
        )
        grad, keep, away = advance(chains, (grad, keep, away))
        chains.append(Chain(scatter_sum(keep, away, slc)))
        grad = advance(chains[-1:], grad)
        both = cond1 + cond2
        grad_silu = both if grad_silu is None else grad_silu + both
    done = [chain.finish() for chain in chains]
    halves = [done[2 * (layers - 1 - layer) + 1] + done[2 * (layers - 1 - layer)] for layer in range(layers)]
    sigmoid_c = jax.nn.sigmoid(condition)
    grad_cond = grad_silu * sigmoid_c * (1.0 + condition * (1.0 - sigmoid_c))
    return (output, grad, grad_cond) + tuple(unpack(halves, cols, owners, layers))


def solution(mesh):
    rows3 = P(("fsdp", "rep"), None, None)
    rows2 = P(("fsdp", "rep"), None)
    pair = (P(None, "fsdp", None), P(None, "fsdp"))
    return jax.shard_map(
        functools.partial(program, Slice(mesh)),
        mesh=mesh,
        in_specs=(rows3, rows2, rows3) + pair * 5,
        out_specs=(rows3, rows3, rows2) + pair * 5,
        check_vma=False,
    )
```
